32 devices in a mesh: grp: 4 (over x, core), ops: 8 (over z, y).
Axes of the slice: x: 2, y: 2, z: 4, core: 2. Of those that a mesh axis runs over, the one named last changes fastest.
Arguments:
- psi: bfloat16 [28, 384, 384], P('grp', 'ops'), may hold values from -6 to 6
- left_ops: bfloat16 [28, 8, 384, 384], P('grp', 'ops'), may hold values from -1 to 2
- right_ops: bfloat16 [28, 8, 384, 384], P('grp', 'ops'), may hold values from -1 to 2
- right_group: int32 [28, 1], replicated, may hold values from 0 to 3; in each aligned block of 7 rows (0 to 6, 7 to 13, ...) at most 2 rows name the same one
- right_slot: int32 [28], replicated, may hold values from 0 to 6
- precond_diag: float32 [28, 384, 384], P('grp', 'ops'), may hold values from 0.25 to 8
Outputs:
- sigma: float32 [28, 384, 384], P('grp', 'ops')
- correction: float32 [28, 384, 384], P('grp', 'ops')
The draws below stay inside these ranges and needn't reach their ends.
Inputs may be any that keep to these rules, and one draw needn't show every extreme that they name: In the 7 sectors of one group, at most 2 have their right_group equal to any one group; some group reaches 2.
All inputs are finite; a program needn't handle non-finite values.
Results may differ from the reference program's by a relative error of at most 0.0006.
The reference program's roundings to bfloat16 on the way (of `image`) count: a program that leaves them out, or rounds other values in their place, can miss the bound.
Values may be sent and summed in bfloat16 or wider, within the bound.
A program may use at most 64 MiB of HBM per device.

```python
import math
import jax
import jax.numpy as jnp
import numpy as np
from jax import lax

SEC = 384
SPG = 7
NSEC = 28
K = 8
CAP = 2
N_GRP = 4


def operator_blocks(key):
    noise = jax.random.normal(key, (NSEC, K, SEC, SEC), jnp.float32)
    return jnp.eye(SEC, dtype=jnp.float32) + 0.5 * noise / math.sqrt(SEC)


def draw_left_ops(key, part):
    return operator_blocks(jax.random.fold_in(key, 11)).astype(jnp.bfloat16)


def draw_right_ops(key, part):
    return (operator_blocks(jax.random.fold_in(key, 23)) / K).astype(jnp.bfloat16)


def plant(result, own_key, least, high):
    spot = [jax.random.randint(jax.random.fold_in(own_key, axis), (), 0, length) for axis, length in enumerate(result.shape)]
    main_axis = result.shape.index(max(result.shape))
    beside = spot[:main_axis] + [(spot[main_axis] + 1) % result.shape[main_axis]] + spot[main_axis + 1:]
    return result.at[tuple(spot)].set(least).at[tuple(beside)].set(high)


def level_of(stream_key, dims, shards, low, largest):
    gain = 1.0
    for axis_at, parts in shards:
        draws = jax.random.uniform(jax.random.fold_in(jax.random.fold_in(stream_key, 6), axis_at), (parts,), jnp.float32, low / len(shards), largest / len(shards))
        gain = gain * jnp.repeat(jnp.exp(draws), dims[axis_at] // parts).reshape((-1,) + (1,) * (len(dims) - 1 - axis_at))
    return gain


def assign_block(key, own, number, rows, amount, top, most, lean):
    order = jax.random.permutation(key, amount)
    packed, ordinary = portions_of(amount, rows * top, most, lean, True), portions_of(amount, rows * top, most, lean, False)
    places = jnp.arange(amount)

    def named(sizes, turn):
        used = int((sizes > 0).sum())
        fixed = max(1, used // 4)
        moved = fixed + (places - fixed + turn * (used - fixed)) % max(1, amount - fixed)
        return jnp.zeros((amount,), jnp.int32).at[order[jnp.where(places < fixed, places, moved)]].set(jnp.asarray(sizes, jnp.int32))

    sizes = jnp.where(number % 4 == 0, named(packed, number // 4), named(ordinary, number - number // 4 - 1))
    mixed = jax.random.permutation(jax.random.fold_in(own, 3), amount)
    source_of, taker = mixed[0:amount // 2 * 2:2], mixed[1:amount // 2 * 2:2]
    margin = jnp.minimum(sizes[source_of] - 1, most - sizes[taker]) // 2
    margin = jnp.where((source_of == order[0]) | (taker == order[0]) | (sizes[taker] == 0), 0, jnp.maximum(margin, 0))
    moved = jax.random.randint(jax.random.fold_in(own, 4), (amount // 2,), 0, 1 << 20) % (margin + 1)
    sizes = sizes.at[source_of].add(-moved).at[taker].add(moved)
    items = jnp.searchsorted(jnp.cumsum(sizes), jnp.arange(rows * top), side="right").astype(jnp.int32)
    table = items.reshape(top, rows).T
    table = table[jax.random.permutation(jax.random.fold_in(own, 1), rows)]
    turn = jax.random.randint(jax.random.fold_in(own, 2), (rows, 1), 0, top)
    return jnp.take_along_axis(table, (jnp.arange(top)[None, :] + turn) % top, axis=1)


def portions_of(number_of, total, bound, slope, full):
    portions = [(1 << 20) // math.isqrt(grade ** slope) + 1 for grade in range(1, number_of + 1)]
    largest = bound if full else min(bound, max(-(-total // number_of), total * portions[0] // sum(portions)))
    least = 1 if total - largest >= number_of - 1 else 0
    holding, surplus = [largest] + [least] * (number_of - 1), total - largest - least * (number_of - 1)
    while surplus > 0:
        candidates = [i for i in range(1, number_of) if holding[i] < largest] or [i for i in range(1, number_of) if holding[i] < bound]
        pool, left = sum([portions[i] for i in candidates]), surplus
        for i in candidates:
            extra = min(bound - holding[i], max(1, left * portions[i] // pool), surplus)
            holding[i] = holding[i] + extra
            surplus = surplus - extra
    return np.array(holding)


def gaussian(stream_key, extent, spread, most, cuts=(), kind=jnp.bfloat16):
    factor_of = level_of(stream_key, extent, cuts, -0.22, 0.18) if cuts else 1.0
    drawn = jax.random.normal(stream_key, extent, jnp.float32) * spread * factor_of
    return jnp.minimum(jnp.maximum(drawn, -most), most).astype(kind)


def setup_inputs(seed: int = 0) -> dict:
    key_list = jax.random.split(jax.random.key(seed), 7)
    psi = gaussian(key_list[0], (NSEC, SEC, SEC), 1.0, 6.0, ((0, 4), (1, 8)))
    left_ops = draw_left_ops(jax.random.fold_in(key_list[6], 71), 0)
    right_ops = draw_right_ops(jax.random.fold_in(key_list[6], 71), 0)
    right_group_keys = jax.random.split(jax.random.fold_in(key_list[3], 1), NSEC // SPG)
    right_group_turns = jax.random.permutation(jax.random.fold_in(key_list[3], 3), NSEC // SPG)
    right_group = jax.vmap(lambda own, number: assign_block(jax.random.fold_in(key_list[3], 2), own, number, SPG, N_GRP, 1, CAP, 2))(right_group_keys, right_group_turns).reshape((NSEC, 1))
    right_slot = plant(jax.random.randint(key_list[4], (NSEC,), 0, SPG), jax.random.fold_in(key_list[4], 1), 0, SPG - 1).astype(jnp.int32)
    precond_diag = jnp.clip(jnp.exp(math.log(8.0) - 3.465736 * jax.random.uniform(key_list[5], (NSEC, SEC, SEC), jnp.float32) ** level_of(key_list[5], (NSEC, SEC, SEC), ((0, 4), (1, 8)), -0.2, 0.2)), 0.25, 8.0)
    return {"psi": psi, "left_ops": left_ops, "right_ops": right_ops, "right_group": right_group, "right_slot": right_slot, "precond_diag": precond_diag}


def reference(psi, left_ops, right_ops, right_group, right_slot, precond_diag):
    partner = (right_group[:, 0] * SPG + right_slot).astype(jnp.int32)

    def sector(index):
        block = psi[index]
        lefts = left_ops[index]
        rights = right_ops[partner[index]]

        def term(total, pair):
            left, right = pair
            image = jnp.dot(block, right.T, preferred_element_type=jnp.float32).astype(jnp.bfloat16)
            return total + jnp.dot(left, image, preferred_element_type=jnp.float32), None

        total, _ = lax.scan(term, jnp.zeros((SEC, SEC), jnp.float32), (lefts, rights))
        return total

    sigma = lax.map(sector, jnp.arange(NSEC, dtype=jnp.int32))
    wave = psi.astype(jnp.float32)
    theta = jnp.sum(wave * sigma) / jnp.sum(wave * wave)
    gap = precond_diag - theta
    correction = (sigma - theta * wave) * gap / (gap * gap + 1.0)
    return sigma, correction
```

```python
import functools

import jax
import jax.numpy as jnp
from jax import lax
from jax.experimental import pallas as pl
from jax.experimental.pallas import tpu as pltpu
from jax.sharding import PartitionSpec as P

MESH = pl.DeviceIdType.MESH
VMEM_BYTES = 60 * 1024 * 1024


def early_sums(whole, partial_value, wave):
    whole_wave = whole.astype(jnp.float32)
    return lax.psum((jnp.sum(whole_wave * partial_value), jnp.sum(wave * wave)), ("grp", "ops"))


def plain_shards(psi, left_ops, right_ops, right_group, right_slot, precond_diag):
    groups = lax.axis_size("grp")
    here = lax.axis_index("grp")
    spg = psi.shape[0]
    cap = (spg + groups - 1) // groups
    owner = right_group[:, 0].reshape(groups, spg)
    slots = right_slot.reshape(groups, spg)
    match = owner == here
    rank = jnp.cumsum(match.astype(jnp.int32), axis=1) - 1
    places = jnp.arange(cap, dtype=jnp.int32)
    pick = match[:, None, :] & (rank[:, None, :] == places[None, :, None])
    source = jnp.sum(jnp.where(pick, slots[:, None, :], 0), axis=2).reshape(-1)
    mine = lax.dynamic_index_in_dim(owner, here, 0, keepdims=False)
    order_ids = jnp.arange(spg, dtype=jnp.int32)
    earlier = (mine[:, None] == mine[None, :]) & (order_ids[None, :] < order_ids[:, None])
    position = mine * cap + jnp.sum(earlier.astype(jnp.int32), axis=1)
    whole = lax.all_gather(psi, "ops", axis=1, tiled=True)
    outgoing = jnp.take(right_ops, source, axis=0)
    incoming = lax.all_to_all(outgoing, "grp", split_axis=0, concat_axis=0, tiled=True)
    partner_blocks = jnp.take(incoming, position, axis=0)
    images = jnp.einsum(
        "jac,jkdc->jkad", whole, partner_blocks, preferred_element_type=jnp.float32
    ).astype(jnp.bfloat16)
    wave = psi.astype(jnp.float32)
    partial_value = jnp.einsum(
        "jkab,jkbd->jad", left_ops, images, preferred_element_type=jnp.float32
    )
    correlation, norm_sq = early_sums(whole, partial_value, wave)
    sigma = lax.psum_scatter(partial_value, "ops", scatter_dimension=1, tiled=True)
    theta = correlation / norm_sq
    gap = precond_diag - theta
    correction = (sigma - theta * wave) * gap / (gap * gap + 1.0)
    return (sigma, correction)


def chunks_of(spg):
    cuts, at = [], 0
    while at < spg:
        size = min(2, spg - at) if spg - at != 3 else 3
        cuts.append((at, size))
        at += size
    return cuts


def fold(value):
    rows, cols = value.shape
    value = jnp.sum(value.reshape(rows // 8, 8, cols), axis=0)
    total = value[:, 0:128]
    for at in range(128, cols, 128):
        total = total + value[:, at:at + 128]
    return total


def kernel(groups, n_z, n_y, cap, rg, rs, psi, left, right, diag, sig_o, cor_o,
           whole, lv, rv, dv, rsend, rrecv, part, yrecv, zacc, zrecv, sigv, corv,
           stat, statz, staty, statg, send_sem, recv_sem, local_sem):
    spg, rows, sec = psi.shape
    g = lax.axis_index("grp")
    o = lax.axis_index("ops")
    z, y = o // n_y, o % n_y
    count = iter(range(1 << 20))
    count_local = iter(range(1 << 20))
    sent = []

    def z_peer(d):
        return {"ops": lax.rem(z + d, n_z) * n_y + y}

    def z_from(d):
        return lax.rem(z + n_z - d, n_z)

    y_peer = {"ops": z * n_y + (n_y - 1 - y)}

    def g_peer(d):
        return {"grp": lax.rem(g + d, groups)}

    def remote(src, dst, device, arrive=None):
        i = next(count)
        copy = pltpu.make_async_remote_copy(
            src_ref=src, dst_ref=dst, send_sem=send_sem.at[i], recv_sem=recv_sem.at[i],
            device_id=device, device_id_type=MESH)
        copy.start()
        sent.append(copy)
        if arrive is None:
            return copy
        return pltpu.make_async_remote_copy(
            src_ref=src, dst_ref=arrive, send_sem=send_sem.at[i], recv_sem=recv_sem.at[i],
            device_id=device, device_id_type=MESH)

    def local(src, dst):
        copy = pltpu.make_async_copy(src, dst, local_sem.at[next(count_local)])
        copy.start()
        return copy

    def rows_of(owner):
        return pl.ds(pl.multiple_of(owner * rows, rows), rows)

    right_in = local(right.at[:, 0], rv)
    psi_in = local(psi, whole.at[:, rows_of(o)])
    left_in = local(left.at[:, 0], lv)
    diag_in = local(diag, dv)

    barrier = pltpu.get_barrier_semaphore()
    peers = [z_peer(d) for d in range(1, n_z)] + [y_peer] + [g_peer(d) for d in range(1, groups)]
    for peer in peers:
        pl.semaphore_signal(barrier, inc=1, device_id=peer, device_id_type=MESH)
    pl.semaphore_wait(barrier, len(peers))

    from_z, from_y = {}, []
    cuts = chunks_of(spg)
    for c, (at, size) in enumerate(cuts):
        src = psi.at[pl.ds(at, size)]
        spot = whole.at[pl.ds(at, size), rows_of(o)]
        from_y.append(remote(src, spot, y_peer,
                             whole.at[pl.ds(at, size), rows_of(z * n_y + n_y - 1 - y)]))
        for d in range(1, n_z):
            from_z[c, d] = remote(src, spot, z_peer(d),
                                  whole.at[pl.ds(at, size), rows_of(z_from(d) * n_y + y)])

    right_in.wait()
    for d in range(groups):
        there = lax.rem(g + d, groups)
        found = jnp.int32(0)
        source = [jnp.int32(0)] * cap
        for j in range(spg):
            match = rg[there * spg + j, 0] == g
            slot = rs[there * spg + j]
            for r in range(cap):
                source[r] = jnp.where(match & (found == r), slot, source[r])
            found = found + match.astype(jnp.int32)
        for r in range(cap):
            if d == 0:
                rrecv[r] = rv[source[r]]
            else:
                rsend[(d - 1) * cap + r] = rv[source[r]]
    from_g = []
    for r in range(cap):
        for d in sorted(range(1, groups), key=lambda d: abs(2 * d - groups)):
            from_g.append(remote(rsend.at[(d - 1) * cap + r], rrecv.at[d * cap + r], g_peer(d)))

    for c, (at, size) in enumerate(cuts):
        for d in range(1, n_z):
            from_z[c, d].wait_recv()
            owner = z_from(d) * n_y
            spot = whole.at[pl.ds(at, size), rows_of(owner + y)]
            from_y.append(remote(spot, spot, y_peer,
                                 whole.at[pl.ds(at, size), rows_of(owner + n_y - 1 - y)]))

    position = []
    mine = [rg[g * spg + j, 0] for j in range(spg)]
    for j in range(spg):
        rank = jnp.int32(0)
        for i in range(j):
            rank = rank + (mine[i] == mine[j]).astype(jnp.int32)
        position.append(lax.rem(g - mine[j] + groups, groups) * cap
                        + jnp.minimum(rank, cap - 1))

    psi_in.wait()
    norm = jnp.zeros((8, 128), jnp.float32)
    for j in range(spg):
        wave = whole[j, rows_of(o), :].astype(jnp.float32)
        norm = norm + fold(wave * wave)
    stat[0, 1] = norm
    left_in.wait()
    for copy in from_g + from_y:
        copy.wait_recv()

    corr = jnp.zeros((8, 128), jnp.float32)
    across = []
    for j in range(spg):
        block = whole[j]
        image = lax.dot_general(block, rrecv[position[j]], (((1,), (1,)), ((), ())),
                                preferred_element_type=jnp.float32).astype(jnp.bfloat16)
        value = jnp.dot(lv[j], image, preferred_element_type=jnp.float32)
        part[j] = value.reshape(n_z, n_y, rows, sec)
        corr = corr + fold(block.astype(jnp.float32) * value)
        across.append(remote(part.at[j, :, n_y - 1 - y], yrecv.at[j], y_peer))
    stat[0, 0] = corr

    def sums_out(stage):
        if stage == 0:
            return [remote(stat.at[0], statz.at[d - 1], z_peer(d)) for d in range(1, n_z)]
        if stage == 1:
            return [remote(stat.at[1], staty.at[0], y_peer)]
        return [remote(stat.at[2], statg.at[d - 1], g_peer(d)) for d in range(1, groups)]

    def sums_in(stage, copies):
        landed = (statz, staty, statg)[stage]
        for copy in copies:
            copy.wait_recv()
        total = stat[stage]
        for i in range(landed.shape[0]):
            total = total + landed[i]
        stat[stage + 1] = total

    sums = sums_out(0)
    diag_in.wait()
    along = []
    outs = []
    theta = None

    def finish(j):
        for copy in along[j]:
            copy.wait_recv()
        sigma = zacc[j, z]
        for d in range(1, n_z):
            sigma = sigma + zrecv[j, d - 1]
        sigv[j] = sigma
        outs.append(local(sigv.at[j], sig_o.at[j]))
        wave = whole[j, rows_of(o), :].astype(jnp.float32)
        gap = dv[j] - theta
        corv[j] = (sigma - theta * wave) * gap / (gap * gap + 1.0)
        outs.append(local(corv.at[j], cor_o.at[j]))

    done = 0
    for j in range(spg):
        across[j].wait_recv()
        for k in range(n_z):
            zacc[j, k] = part[j, k, y] + yrecv[j, k]
        along.append([remote(zacc.at[j, lax.rem(z + d, n_z)], zrecv.at[j, d - 1], z_peer(d))
                      for d in range(1, n_z)])
        if j < 3:
            sums_in(j, sums)
            if j < 2:
                sums = sums_out(j + 1)
            else:
                theta = jnp.sum(stat[3, 0]) / jnp.sum(stat[3, 1])
        elif j >= 4:
            finish(done)
            done += 1
    while done < spg:
        finish(done)
        done += 1
    for copy in sent:
        copy.wait_send()
    for copy in outs:
        copy.wait()


def fused_shards(psi, left_ops, right_ops, right_group, right_slot, precond_diag):
    groups = lax.axis_size("grp")
    n_y = 2
    n_z = lax.axis_size("ops") // n_y
    spg, rows, sec = psi.shape
    cap = (spg + groups - 1) // groups
    f32, bf16 = jnp.float32, jnp.bfloat16
    cuts = len(chunks_of(spg))
    copies = cuts * (2 * n_z - 1) + (groups - 1) * cap + spg * n_z + (n_z - 1) + 1 + (groups - 1)
    shape = jax.ShapeDtypeStruct((spg, rows, sec), f32)
    return pl.pallas_call(
        functools.partial(kernel, groups, n_z, n_y, cap),
        out_shape=(shape, shape),
        in_specs=[pl.BlockSpec(memory_space=pltpu.SMEM)] * 2 + [pl.BlockSpec(memory_space=pl.ANY)] * 4,
        out_specs=(pl.BlockSpec(memory_space=pl.ANY),) * 2,
        scratch_shapes=[
            pltpu.VMEM((spg, sec, sec), bf16),
            pltpu.VMEM((spg, sec, sec), bf16),
            pltpu.VMEM((spg, sec, sec), bf16),
            pltpu.VMEM((spg, rows, sec), f32),
            pltpu.VMEM(((groups - 1) * cap, sec, sec), bf16),
            pltpu.VMEM((groups * cap, sec, sec), bf16),
            pltpu.VMEM((spg, n_z, n_y, rows, sec), f32),
            pltpu.VMEM((spg, n_z, rows, sec), f32),
            pltpu.VMEM((spg, n_z, rows, sec), f32),
            pltpu.VMEM((spg, n_z - 1, rows, sec), f32),
            pltpu.VMEM((spg, rows, sec), f32),
            pltpu.VMEM((spg, rows, sec), f32),
            pltpu.VMEM((4, 2, 8, 128), f32),
            pltpu.VMEM((n_z - 1, 2, 8, 128), f32),
            pltpu.VMEM((1, 2, 8, 128), f32),
            pltpu.VMEM((groups - 1, 2, 8, 128), f32),
            pltpu.SemaphoreType.DMA((copies,)),
            pltpu.SemaphoreType.DMA((copies,)),
            pltpu.SemaphoreType.DMA((4 + 2 * spg,)),
        ],
        compiler_params=pltpu.CompilerParams(
            collective_id=0, has_side_effects=True, vmem_limit_bytes=VMEM_BYTES),
    )(right_group, right_slot, psi, left_ops, right_ops, precond_diag)


def shards(psi, left_ops, right_ops, right_group, right_slot, precond_diag):
    spg, rows, sec = psi.shape
    groups, ops = lax.axis_size("grp"), lax.axis_size("ops")
    cap = (spg + groups - 1) // groups
    held = sec * sec * (2 * (3 * spg + (2 * groups - 1) * cap) + 4 * (3 * spg))
    fits = (rows % 16 == 0 and sec % 128 == 0 and ops % 2 == 0 and ops > 2 and groups > 1
            and spg > 3 and left_ops.shape[1] == 1 and held < 40 * 1024 * 1024)
    form = fused_shards if fits else plain_shards
    return form(psi, left_ops, right_ops, right_group, right_slot, precond_diag)


def solution(mesh):
    in_specs = (
        P("grp", "ops", None),
        P("grp", "ops", None, None),
        P("grp", "ops", None, None),
        P(),
        P(),
        P("grp", "ops", None),
    )
    out_specs = (P("grp", "ops", None), P("grp", "ops", None))
    return jax.shard_map(shards, mesh=mesh, in_specs=in_specs, out_specs=out_specs, check_vma=False)
```

```python
import functools

import jax
import jax.numpy as jnp
from jax import lax
from jax.experimental import pallas as pl
from jax.experimental.pallas import tpu as pltpu
from jax.sharding import PartitionSpec as P

MESH = pl.DeviceIdType.MESH
VMEM_BYTES = 60 * 1024 * 1024
AHEAD = 3
LATE = 4


def early_sums(whole, partial_value, wave):
    whole_wave = whole.astype(jnp.float32)
    return lax.psum((jnp.sum(whole_wave * partial_value), jnp.sum(wave * wave)), ("grp", "ops"))


def plain_shards(psi, left_ops, right_ops, right_group, right_slot, precond_diag):
    groups = lax.axis_size("grp")
    here = lax.axis_index("grp")
    spg = psi.shape[0]
    cap = (spg + groups - 1) // groups
    owner = right_group[:, 0].reshape(groups, spg)
    slots = right_slot.reshape(groups, spg)
    match = owner == here
    rank = jnp.cumsum(match.astype(jnp.int32), axis=1) - 1
    places = jnp.arange(cap, dtype=jnp.int32)
    pick = match[:, None, :] & (rank[:, None, :] == places[None, :, None])
    source = jnp.sum(jnp.where(pick, slots[:, None, :], 0), axis=2).reshape(-1)
    mine = lax.dynamic_index_in_dim(owner, here, 0, keepdims=False)
    order_ids = jnp.arange(spg, dtype=jnp.int32)
    earlier = (mine[:, None] == mine[None, :]) & (order_ids[None, :] < order_ids[:, None])
    position = mine * cap + jnp.sum(earlier.astype(jnp.int32), axis=1)
    whole = lax.all_gather(psi, "ops", axis=1, tiled=True)
    outgoing = jnp.take(right_ops, source, axis=0)
    incoming = lax.all_to_all(outgoing, "grp", split_axis=0, concat_axis=0, tiled=True)
    partner_blocks = jnp.take(incoming, position, axis=0)
    images = jnp.einsum(
        "jac,jkdc->jkad", whole, partner_blocks, preferred_element_type=jnp.float32
    ).astype(jnp.bfloat16)
    wave = psi.astype(jnp.float32)
    partial_value = jnp.einsum(
        "jkab,jkbd->jad", left_ops, images, preferred_element_type=jnp.float32
    )
    correlation, norm_sq = early_sums(whole, partial_value, wave)
    sigma = lax.psum_scatter(partial_value, "ops", scatter_dimension=1, tiled=True)
    theta = correlation / norm_sq
    gap = precond_diag - theta
    correction = (sigma - theta * wave) * gap / (gap * gap + 1.0)
    return (sigma, correction)


def chunks_of(spg):
    cuts, at = [], 0
    while at < spg:
        size = min(2, spg - at) if spg - at != 3 else 3
        cuts.append((at, size))
        at += size
    return cuts


def fold(value):
    rows, cols = value.shape
    value = jnp.sum(value.reshape(rows // 8, 8, cols), axis=0)
    total = value[:, 0:128]
    for at in range(128, cols, 128):
        total = total + value[:, at:at + 128]
    return total


def kernel(groups, n_z, n_y, cap, rg, rs, psi, left, right, diag, sig_o, cor_o,
           whole, lv, rv, dv, rsend, rrecv, part, yrecv, zacc, zrecv, sigv, corv,
           stat, statz, staty, statg, send_sem, recv_sem, local_sem):
    spg, rows, sec = psi.shape
    g = lax.axis_index("grp")
    o = lax.axis_index("ops")
    z, y = o // n_y, o % n_y
    count = iter(range(1 << 20))
    count_local = iter(range(1 << 20))
    sent = []

    def z_peer(d):
        return {"ops": lax.rem(z + d, n_z) * n_y + y}

    def z_from(d):
        return lax.rem(z + n_z - d, n_z)

    y_peer = {"ops": z * n_y + (n_y - 1 - y)}

    def g_peer(d):
        return {"grp": lax.rem(g + d, groups)}

    def remote(src, dst, device, arrive=None):
        i = next(count)
        copy = pltpu.make_async_remote_copy(
            src_ref=src, dst_ref=dst, send_sem=send_sem.at[i], recv_sem=recv_sem.at[i],
            device_id=device, device_id_type=MESH)
        copy.start()
        sent.append(copy)
        if arrive is None:
            return copy
        return pltpu.make_async_remote_copy(
            src_ref=src, dst_ref=arrive, send_sem=send_sem.at[i], recv_sem=recv_sem.at[i],
            device_id=device, device_id_type=MESH)

    def local(src, dst):
        copy = pltpu.make_async_copy(src, dst, local_sem.at[next(count_local)])
        copy.start()
        return copy

    def rows_of(owner):
        return pl.ds(pl.multiple_of(owner * rows, rows), rows)

    right_in = local(right.at[:, 0], rv)
    psi_in = local(psi, whole.at[:, rows_of(o)])
    left_in = local(left.at[:, 0], lv)
    diag_in = local(diag, dv)

    barrier = pltpu.get_barrier_semaphore()
    peers = [z_peer(d) for d in range(1, n_z)] + [y_peer] + [g_peer(d) for d in range(1, groups)]
    for peer in peers:
        pl.semaphore_signal(barrier, inc=1, device_id=peer, device_id_type=MESH)
    pl.semaphore_wait(barrier, len(peers))

    from_z, from_y = {}, []
    cuts = chunks_of(spg)
    for c, (at, size) in enumerate(cuts):
        src = psi.at[pl.ds(at, size)]
        spot = whole.at[pl.ds(at, size), rows_of(o)]
        from_y.append(remote(src, spot, y_peer,
                             whole.at[pl.ds(at, size), rows_of(z * n_y + n_y - 1 - y)]))
        for d in range(1, n_z):
            from_z[c, d] = remote(src, spot, z_peer(d),
                                  whole.at[pl.ds(at, size), rows_of(z_from(d) * n_y + y)])

    right_in.wait()
    for d in range(groups):
        there = lax.rem(g + d, groups)
        found = jnp.int32(0)
        source = [jnp.int32(0)] * cap
        for j in range(spg):
            match = rg[there * spg + j] == g
            slot = rs[there * spg + j]
            for r in range(cap):
                source[r] = jnp.where(match & (found == r), slot, source[r])
            found = found + match.astype(jnp.int32)
        for r in range(cap):
            if d == 0:
                rrecv[r] = rv[source[r]]
            else:
                rsend[(d - 1) * cap + r] = rv[source[r]]
    from_g = []
    for r in range(cap):
        for d in sorted(range(1, groups), key=lambda d: abs(2 * d - groups)):
            from_g.append(remote(rsend.at[(d - 1) * cap + r], rrecv.at[d * cap + r], g_peer(d)))

    for c, (at, size) in enumerate(cuts):
        for d in range(1, n_z):
            from_z[c, d].wait_recv()
            owner = z_from(d) * n_y
            spot = whole.at[pl.ds(at, size), rows_of(owner + y)]
            from_y.append(remote(spot, spot, y_peer,
                                 whole.at[pl.ds(at, size), rows_of(owner + n_y - 1 - y)]))

    position = []
    mine = [rg[g * spg + j] for j in range(spg)]
    for j in range(spg):
        rank = jnp.int32(0)
        for i in range(j):
            rank = rank + (mine[i] == mine[j]).astype(jnp.int32)
        position.append(lax.rem(g - mine[j] + groups, groups) * cap
                        + jnp.minimum(rank, cap - 1))

    psi_in.wait()
    norm = jnp.zeros((8, 128), jnp.float32)
    for j in range(spg):
        wave = whole[j, rows_of(o), :].astype(jnp.float32)
        norm = norm + fold(wave * wave)
    stat[0, 1] = norm
    left_in.wait()
    for copy in from_g + from_y:
        copy.wait_recv()

    corr = jnp.zeros((8, 128), jnp.float32)
    across = []

    def y_out(j):
        return remote(part.at[j, :, n_y - 1 - y], yrecv.at[j], y_peer)

    for j in range(spg):
        block = whole[j]
        image = lax.dot_general(block, rrecv[position[j]], (((1,), (1,)), ((), ())),
                                preferred_element_type=jnp.float32).astype(jnp.bfloat16)
        value = jnp.dot(lv[j], image, preferred_element_type=jnp.float32)
        part[j] = value.reshape(n_z, n_y, rows, sec)
        corr = corr + fold(block.astype(jnp.float32) * value)
        if j < AHEAD:
            across.append(y_out(j))
    stat[0, 0] = corr

    def sums_out(stage):
        if stage == 0:
            return [remote(stat.at[0], statg.at[d - 1], g_peer(d)) for d in range(1, groups)]
        if stage == 1:
            return [remote(stat.at[1], statz.at[d - 1], z_peer(d)) for d in range(1, n_z)]
        return [remote(stat.at[2], staty.at[0], y_peer)]

    def sums_in(stage, copies):
        landed = (statg, statz, staty)[stage]
        for copy in copies:
            copy.wait_recv()
        total = stat[stage]
        for i in range(landed.shape[0]):
            total = total + landed[i]
        stat[stage + 1] = total

    sums = sums_out(0)
    diag_in.wait()
    along = []
    outs = []
    theta = None

    def finish(j):
        for copy in along[j]:
            copy.wait_recv()
        sigma = zacc[j, z]
        for d in range(1, n_z):
            sigma = sigma + zrecv[j, d - 1]
        sigv[j] = sigma
        outs.append(local(sigv.at[j], sig_o.at[j]))
        wave = whole[j, rows_of(o), :].astype(jnp.float32)
        gap = dv[j] - theta
        corv[j] = (sigma - theta * wave) * gap / (gap * gap + 1.0)
        outs.append(local(corv.at[j], cor_o.at[j]))

    done = 0
    for j in range(spg):
        across[j].wait_recv()
        if j < 2:
            sums_in(j, sums)
            sums = sums_out(j + 1)
        elif j == LATE:
            sums_in(2, sums)
            theta = jnp.sum(stat[3, 0]) / jnp.sum(stat[3, 1])
        if j + AHEAD < spg:
            across.append(y_out(j + AHEAD))
        for k in range(n_z):
            zacc[j, k] = part[j, k, y] + yrecv[j, k]
        along.append([remote(zacc.at[j, lax.rem(z + d, n_z)], zrecv.at[j, d - 1], z_peer(d))
                      for d in range(1, n_z)])
        if j > LATE:
            finish(done)
            done += 1
    while done < spg:
        finish(done)
        done += 1
    for copy in sent:
        copy.wait_send()
    for copy in outs:
        copy.wait()


def fused_shards(psi, left_ops, right_ops, right_group, right_slot, precond_diag):
    groups = lax.axis_size("grp")
    n_y = 2
    n_z = lax.axis_size("ops") // n_y
    spg, rows, sec = psi.shape
    cap = (spg + groups - 1) // groups
    f32, bf16 = jnp.float32, jnp.bfloat16
    cuts = len(chunks_of(spg))
    copies = cuts * (2 * n_z - 1) + (groups - 1) * cap + spg * n_z + (n_z - 1) + 1 + (groups - 1)
    shape = jax.ShapeDtypeStruct((spg, rows, sec), f32)
    return pl.pallas_call(
        functools.partial(kernel, groups, n_z, n_y, cap),
        out_shape=(shape, shape),
        in_specs=[pl.BlockSpec(memory_space=pltpu.SMEM)] * 2 + [pl.BlockSpec(memory_space=pl.ANY)] * 4,
        out_specs=(pl.BlockSpec(memory_space=pl.ANY),) * 2,
        scratch_shapes=[
            pltpu.VMEM((spg, sec, sec), bf16),
            pltpu.VMEM((spg, sec, sec), bf16),
            pltpu.VMEM((spg, sec, sec), bf16),
            pltpu.VMEM((spg, rows, sec), f32),
            pltpu.VMEM(((groups - 1) * cap, sec, sec), bf16),
            pltpu.VMEM((groups * cap, sec, sec), bf16),
            pltpu.VMEM((spg, n_z, n_y, rows, sec), f32),
            pltpu.VMEM((spg, n_z, rows, sec), f32),
            pltpu.VMEM((spg, n_z, rows, sec), f32),
            pltpu.VMEM((spg, n_z - 1, rows, sec), f32),
            pltpu.VMEM((spg, rows, sec), f32),
            pltpu.VMEM((spg, rows, sec), f32),
            pltpu.VMEM((4, 2, 8, 128), f32),
            pltpu.VMEM((n_z - 1, 2, 8, 128), f32),
            pltpu.VMEM((1, 2, 8, 128), f32),
            pltpu.VMEM((groups - 1, 2, 8, 128), f32),
            pltpu.SemaphoreType.DMA((copies,)),
            pltpu.SemaphoreType.DMA((copies,)),
            pltpu.SemaphoreType.DMA((4 + 2 * spg,)),
        ],
        compiler_params=pltpu.CompilerParams(
            collective_id=0, has_side_effects=True, vmem_limit_bytes=VMEM_BYTES),
    )(right_group.reshape(-1), right_slot, psi, left_ops, right_ops, precond_diag)


def shards(psi, left_ops, right_ops, right_group, right_slot, precond_diag):
    spg, rows, sec = psi.shape
    groups, ops = lax.axis_size("grp"), lax.axis_size("ops")
    cap = (spg + groups - 1) // groups
    held = sec * sec * (2 * (3 * spg + (2 * groups - 1) * cap) + 4 * (3 * spg))
    fits = (rows % 16 == 0 and sec % 128 == 0 and ops % 2 == 0 and ops > 2 and groups > 1
            and spg > LATE and left_ops.shape[1] == 1 and held < 40 * 1024 * 1024)
    form = fused_shards if fits else plain_shards
    return form(psi, left_ops, right_ops, right_group, right_slot, precond_diag)


def solution(mesh):
    in_specs = (
        P("grp", "ops", None),
        P("grp", "ops", None, None),
        P("grp", "ops", None, None),
        P(),
        P(),
        P("grp", "ops", None),
    )
    out_specs = (P("grp", "ops", None), P("grp", "ops", None))
    return jax.shard_map(shards, mesh=mesh, in_specs=in_specs, out_specs=out_specs, check_vma=False)
```

```python
import functools

import jax
import jax.numpy as jnp
from jax import lax
from jax.experimental import pallas as pl
from jax.experimental.pallas import tpu as pltpu
from jax.sharding import PartitionSpec as P

MESH = pl.DeviceIdType.MESH
VMEM_BYTES = 60 * 1024 * 1024
AHEAD = 3
LATE = 4


def early_sums(whole, partial_value, wave):
    whole_wave = whole.astype(jnp.float32)
    return lax.psum((jnp.sum(whole_wave * partial_value), jnp.sum(wave * wave)), ("grp", "ops"))


def plain_shards(psi, left_ops, right_ops, right_group, right_slot, precond_diag):
    groups = lax.axis_size("grp")
    here = lax.axis_index("grp")
    spg = psi.shape[0]
    cap = (spg + groups - 1) // groups
    owner = right_group[:, 0].reshape(groups, spg)
    slots = right_slot.reshape(groups, spg)
    match = owner == here
    rank = jnp.cumsum(match.astype(jnp.int32), axis=1) - 1
    places = jnp.arange(cap, dtype=jnp.int32)
    pick = match[:, None, :] & (rank[:, None, :] == places[None, :, None])
    source = jnp.sum(jnp.where(pick, slots[:, None, :], 0), axis=2).reshape(-1)
    mine = lax.dynamic_index_in_dim(owner, here, 0, keepdims=False)
    order_ids = jnp.arange(spg, dtype=jnp.int32)
    earlier = (mine[:, None] == mine[None, :]) & (order_ids[None, :] < order_ids[:, None])
    position = mine * cap + jnp.sum(earlier.astype(jnp.int32), axis=1)
    whole = lax.all_gather(psi, "ops", axis=1, tiled=True)
    outgoing = jnp.take(right_ops, source, axis=0)
    incoming = lax.all_to_all(outgoing, "grp", split_axis=0, concat_axis=0, tiled=True)
    partner_blocks = jnp.take(incoming, position, axis=0)
    images = jnp.einsum(
        "jac,jkdc->jkad", whole, partner_blocks, preferred_element_type=jnp.float32
    ).astype(jnp.bfloat16)
    wave = psi.astype(jnp.float32)
    partial_value = jnp.einsum(
        "jkab,jkbd->jad", left_ops, images, preferred_element_type=jnp.float32
    )
    correlation, norm_sq = early_sums(whole, partial_value, wave)
    sigma = lax.psum_scatter(partial_value, "ops", scatter_dimension=1, tiled=True)
    theta = correlation / norm_sq
    gap = precond_diag - theta
    correction = (sigma - theta * wave) * gap / (gap * gap + 1.0)
    return (sigma, correction)


def chunks_of(spg):
    cuts, at = [], 0
    while at < spg:
        size = min(2, spg - at) if spg - at != 3 else 3
        cuts.append((at, size))
        at += size
    return cuts


def fold(value):
    rows, cols = value.shape
    value = jnp.sum(value.reshape(rows // 8, 8, cols), axis=0)
    total = value[:, 0:128]
    for at in range(128, cols, 128):
        total = total + value[:, at:at + 128]
    return total


def coded(value):
    top = jnp.maximum(jnp.max(jnp.abs(value), axis=-2, keepdims=True), 1e-30)
    code = jnp.round(value * (32767.0 / top)).astype(jnp.int32).astype(jnp.int16)
    return code, top * (1.0 / 32767.0)


def decoded(code, step):
    return code.astype(jnp.int32).astype(jnp.float32) * step


def kernel(groups, n_z, n_y, cap, rg, rs, psi, left, right, diag, sig_o, cor_o,
           whole, lv, rv, dv, rsend, rrecv, part, ycode, ystep, yrecv, ysrecv, zcode, zstep, zacc,
           zrecv, zsrecv, sigv, corv,
           stat, statz, staty, statg, send_sem, recv_sem, local_sem):
    spg, rows, sec = psi.shape
    g = lax.axis_index("grp")
    o = lax.axis_index("ops")
    z, y = o // n_y, o % n_y
    count = iter(range(1 << 20))
    count_local = iter(range(1 << 20))
    sent = []

    def z_peer(d):
        return {"ops": lax.rem(z + d, n_z) * n_y + y}

    def z_from(d):
        return lax.rem(z + n_z - d, n_z)

    y_peer = {"ops": z * n_y + (n_y - 1 - y)}

    def g_peer(d):
        return {"grp": lax.rem(g + d, groups)}

    def remote(src, dst, device, arrive=None):
        i = next(count)
        copy = pltpu.make_async_remote_copy(
            src_ref=src, dst_ref=dst, send_sem=send_sem.at[i], recv_sem=recv_sem.at[i],
            device_id=device, device_id_type=MESH)
        copy.start()
        sent.append(copy)
        if arrive is None:
            return copy
        return pltpu.make_async_remote_copy(
            src_ref=src, dst_ref=arrive, send_sem=send_sem.at[i], recv_sem=recv_sem.at[i],
            device_id=device, device_id_type=MESH)

    def local(src, dst):
        copy = pltpu.make_async_copy(src, dst, local_sem.at[next(count_local)])
        copy.start()
        return copy

    def rows_of(owner):
        return pl.ds(pl.multiple_of(owner * rows, rows), rows)

    right_in = local(right.at[:, 0], rv)
    psi_in = local(psi, whole.at[:, rows_of(o)])
    left_in = local(left.at[:, 0], lv)
    diag_in = local(diag, dv)

    barrier = pltpu.get_barrier_semaphore()
    peers = [z_peer(d) for d in range(1, n_z)] + [y_peer] + [g_peer(d) for d in range(1, groups)]
    for peer in peers:
        pl.semaphore_signal(barrier, inc=1, device_id=peer, device_id_type=MESH)
    pl.semaphore_wait(barrier, len(peers))

    from_z, from_y = {}, []
    cuts = chunks_of(spg)
    for c, (at, size) in enumerate(cuts):
        src = psi.at[pl.ds(at, size)]
        spot = whole.at[pl.ds(at, size), rows_of(o)]
        from_y.append(remote(src, spot, y_peer,
                             whole.at[pl.ds(at, size), rows_of(z * n_y + n_y - 1 - y)]))
        for d in range(1, n_z):
            from_z[c, d] = remote(src, spot, z_peer(d),
                                  whole.at[pl.ds(at, size), rows_of(z_from(d) * n_y + y)])

    right_in.wait()
    for d in range(groups):
        there = lax.rem(g + d, groups)
        found = jnp.int32(0)
        source = [jnp.int32(0)] * cap
        for j in range(spg):
            match = rg[there * spg + j] == g
            slot = rs[there * spg + j]
            for r in range(cap):
                source[r] = jnp.where(match & (found == r), slot, source[r])
            found = found + match.astype(jnp.int32)
        for r in range(cap):
            if d == 0:
                rrecv[r] = rv[source[r]]
            else:
                rsend[(d - 1) * cap + r] = rv[source[r]]
    from_g = []
    for r in range(cap):
        for d in sorted(range(1, groups), key=lambda d: abs(2 * d - groups)):
            from_g.append(remote(rsend.at[(d - 1) * cap + r], rrecv.at[d * cap + r], g_peer(d)))

    for c, (at, size) in enumerate(cuts):
        for d in range(1, n_z):
            from_z[c, d].wait_recv()
            owner = z_from(d) * n_y
            spot = whole.at[pl.ds(at, size), rows_of(owner + y)]
            from_y.append(remote(spot, spot, y_peer,
                                 whole.at[pl.ds(at, size), rows_of(owner + n_y - 1 - y)]))

    position = []
    mine = [rg[g * spg + j] for j in range(spg)]
    for j in range(spg):
        rank = jnp.int32(0)
        for i in range(j):
            rank = rank + (mine[i] == mine[j]).astype(jnp.int32)
        position.append(lax.rem(g - mine[j] + groups, groups) * cap
                        + jnp.minimum(rank, cap - 1))

    psi_in.wait()
    norm = jnp.zeros((8, 128), jnp.float32)
    for j in range(spg):
        wave = whole[j, rows_of(o), :].astype(jnp.float32)
        norm = norm + fold(wave * wave)
    stat[0, 1] = norm
    left_in.wait()
    for copy in from_g + from_y:
        copy.wait_recv()

    corr = jnp.zeros((8, 128), jnp.float32)
    across = []

    def y_out(j):
        return [remote(ystep.at[j], ysrecv.at[j], y_peer),
                remote(ycode.at[j], yrecv.at[j], y_peer)]

    for j in range(spg):
        block = whole[j]
        image = lax.dot_general(block, rrecv[position[j]], (((1,), (1,)), ((), ())),
                                preferred_element_type=jnp.float32).astype(jnp.bfloat16)
        value = jnp.dot(lv[j], image, preferred_element_type=jnp.float32)
        part[j] = value.reshape(n_z, n_y, rows, sec)
        ycode[j], ystep[j] = coded(part[j, :, n_y - 1 - y])
        corr = corr + fold(block.astype(jnp.float32) * value)
        if j < AHEAD:
            across.append(y_out(j))
    stat[0, 0] = corr

    def sums_out(stage):
        if stage == 0:
            return [remote(stat.at[0], statg.at[d - 1], g_peer(d)) for d in range(1, groups)]
        if stage == 1:
            return [remote(stat.at[1], statz.at[d - 1], z_peer(d)) for d in range(1, n_z)]
        return [remote(stat.at[2], staty.at[0], y_peer)]

    def sums_in(stage, copies):
        landed = (statg, statz, staty)[stage]
        for copy in copies:
            copy.wait_recv()
        total = stat[stage]
        for i in range(landed.shape[0]):
            total = total + landed[i]
        stat[stage + 1] = total

    sums = sums_out(0)
    diag_in.wait()
    along = []
    outs = []
    theta = None

    def finish(j):
        for copy in along[j]:
            copy.wait_recv()
        sigma = zacc[j, z]
        for d in range(1, n_z):
            sigma = sigma + decoded(zrecv[j, d - 1], zsrecv[j, d - 1])
        sigv[j] = sigma
        outs.append(local(sigv.at[j], sig_o.at[j]))
        wave = whole[j, rows_of(o), :].astype(jnp.float32)
        gap = dv[j] - theta
        corv[j] = (sigma - theta * wave) * gap / (gap * gap + 1.0)
        outs.append(local(corv.at[j], cor_o.at[j]))

    done = 0
    for j in range(spg):
        for copy in across[j]:
            copy.wait_recv()
        if j < 2:
            sums_in(j, sums)
            sums = sums_out(j + 1)
        elif j == LATE:
            sums_in(2, sums)
            theta = jnp.sum(stat[3, 0]) / jnp.sum(stat[3, 1])
        if j + AHEAD < spg:
            across.append(y_out(j + AHEAD))
        total = part[j, :, y] + decoded(yrecv[j], ysrecv[j])
        zacc[j] = total
        zcode[j], zstep[j] = coded(total)
        along.append([])
        for d in range(1, n_z):
            there = lax.rem(z + d, n_z)
            along[j].append(remote(zstep.at[j, there], zsrecv.at[j, d - 1], z_peer(d)))
            along[j].append(remote(zcode.at[j, there], zrecv.at[j, d - 1], z_peer(d)))
        if j > LATE:
            finish(done)
            done += 1
    while done < spg:
        finish(done)
        done += 1
    for copy in sent:
        copy.wait_send()
    for copy in outs:
        copy.wait()


def fused_shards(psi, left_ops, right_ops, right_group, right_slot, precond_diag):
    groups = lax.axis_size("grp")
    n_y = 2
    n_z = lax.axis_size("ops") // n_y
    spg, rows, sec = psi.shape
    cap = (spg + groups - 1) // groups
    f32, bf16, i16 = jnp.float32, jnp.bfloat16, jnp.int16
    cuts = len(chunks_of(spg))
    copies = cuts * (2 * n_z - 1) + (groups - 1) * cap + 2 * spg * n_z + (n_z - 1) + 1 + (groups - 1)
    shape = jax.ShapeDtypeStruct((spg, rows, sec), f32)
    return pl.pallas_call(
        functools.partial(kernel, groups, n_z, n_y, cap),
        out_shape=(shape, shape),
        in_specs=[pl.BlockSpec(memory_space=pltpu.SMEM)] * 2 + [pl.BlockSpec(memory_space=pl.ANY)] * 4,
        out_specs=(pl.BlockSpec(memory_space=pl.ANY),) * 2,
        scratch_shapes=[
            pltpu.VMEM((spg, sec, sec), bf16),
            pltpu.VMEM((spg, sec, sec), bf16),
            pltpu.VMEM((spg, sec, sec), bf16),
            pltpu.VMEM((spg, rows, sec), f32),
            pltpu.VMEM(((groups - 1) * cap, sec, sec), bf16),
            pltpu.VMEM((groups * cap, sec, sec), bf16),
            pltpu.VMEM((spg, n_z, n_y, rows, sec), f32),
            pltpu.VMEM((spg, n_z, rows, sec), i16),
            pltpu.VMEM((spg, n_z, 1, sec), f32),
            pltpu.VMEM((spg, n_z, rows, sec), i16),
            pltpu.VMEM((spg, n_z, 1, sec), f32),
            pltpu.VMEM((spg, n_z, rows, sec), i16),
            pltpu.VMEM((spg, n_z, 1, sec), f32),
            pltpu.VMEM((spg, n_z, rows, sec), f32),
            pltpu.VMEM((spg, n_z - 1, rows, sec), i16),
            pltpu.VMEM((spg, n_z - 1, 1, sec), f32),
            pltpu.VMEM((spg, rows, sec), f32),
            pltpu.VMEM((spg, rows, sec), f32),
            pltpu.VMEM((4, 2, 8, 128), f32),
            pltpu.VMEM((n_z - 1, 2, 8, 128), f32),
            pltpu.VMEM((1, 2, 8, 128), f32),
            pltpu.VMEM((groups - 1, 2, 8, 128), f32),
            pltpu.SemaphoreType.DMA((copies,)),
            pltpu.SemaphoreType.DMA((copies,)),
            pltpu.SemaphoreType.DMA((4 + 2 * spg,)),
        ],
        compiler_params=pltpu.CompilerParams(
            collective_id=0, has_side_effects=True, vmem_limit_bytes=VMEM_BYTES),
    )(right_group.reshape(-1), right_slot, psi, left_ops, right_ops, precond_diag)


def shards(psi, left_ops, right_ops, right_group, right_slot, precond_diag):
    spg, rows, sec = psi.shape
    groups, ops = lax.axis_size("grp"), lax.axis_size("ops")
    cap = (spg + groups - 1) // groups
    held = sec * sec * (2 * (3 * spg + (2 * groups - 1) * cap) + 4 * (3 * spg))
    fits = (rows % 16 == 0 and sec % 128 == 0 and ops % 2 == 0 and ops > 2 and groups > 1
            and spg > LATE and left_ops.shape[1] == 1 and held < 40 * 1024 * 1024)
    form = fused_shards if fits else plain_shards
    return form(psi, left_ops, right_ops, right_group, right_slot, precond_diag)


def solution(mesh):
    in_specs = (
        P("grp", "ops", None),
        P("grp", "ops", None, None),
        P("grp", "ops", None, None),
        P(),
        P(),
        P("grp", "ops", None),
    )
    out_specs = (P("grp", "ops", None), P("grp", "ops", None))
    return jax.shard_map(shards, mesh=mesh, in_specs=in_specs, out_specs=out_specs, check_vma=False)
```

```python
import functools

import jax
import jax.numpy as jnp
from jax import lax
from jax.experimental import pallas as pl
from jax.experimental.pallas import tpu as pltpu
from jax.sharding import PartitionSpec as P

MESH = pl.DeviceIdType.MESH
VMEM_BYTES = 60 * 1024 * 1024
AHEAD = 3
LATE = 4


def early_sums(whole, partial_value, wave):
    whole_wave = whole.astype(jnp.float32)
    return lax.psum((jnp.sum(whole_wave * partial_value), jnp.sum(wave * wave)), ("grp", "ops"))


def plain_shards(psi, left_ops, right_ops, right_group, right_slot, precond_diag):
    groups = lax.axis_size("grp")
    here = lax.axis_index("grp")
    spg = psi.shape[0]
    cap = (spg + groups - 1) // groups
    owner = right_group[:, 0].reshape(groups, spg)
    slots = right_slot.reshape(groups, spg)
    match = owner == here
    rank = jnp.cumsum(match.astype(jnp.int32), axis=1) - 1
    places = jnp.arange(cap, dtype=jnp.int32)
    pick = match[:, None, :] & (rank[:, None, :] == places[None, :, None])
    source = jnp.sum(jnp.where(pick, slots[:, None, :], 0), axis=2).reshape(-1)
    mine = lax.dynamic_index_in_dim(owner, here, 0, keepdims=False)
    order_ids = jnp.arange(spg, dtype=jnp.int32)
    earlier = (mine[:, None] == mine[None, :]) & (order_ids[None, :] < order_ids[:, None])
    position = mine * cap + jnp.sum(earlier.astype(jnp.int32), axis=1)
    whole = lax.all_gather(psi, "ops", axis=1, tiled=True)
    outgoing = jnp.take(right_ops, source, axis=0)
    incoming = lax.all_to_all(outgoing, "grp", split_axis=0, concat_axis=0, tiled=True)
    partner_blocks = jnp.take(incoming, position, axis=0)
    images = jnp.einsum(
        "jac,jkdc->jkad", whole, partner_blocks, preferred_element_type=jnp.float32
    ).astype(jnp.bfloat16)
    wave = psi.astype(jnp.float32)
    partial_value = jnp.einsum(
        "jkab,jkbd->jad", left_ops, images, preferred_element_type=jnp.float32
    )
    correlation, norm_sq = early_sums(whole, partial_value, wave)
    sigma = lax.psum_scatter(partial_value, "ops", scatter_dimension=1, tiled=True)
    theta = correlation / norm_sq
    gap = precond_diag - theta
    correction = (sigma - theta * wave) * gap / (gap * gap + 1.0)
    return (sigma, correction)


def correct(sums, sigma, psi, diag, sig_o, cor_o):
    theta = jnp.sum(sums[0]) / jnp.sum(sums[1])
    for j in range(sigma.shape[0]):
        value = sigma[j]
        sig_o[j] = value
        gap = diag[j] - theta
        cor_o[j] = (value - theta * psi[j].astype(jnp.float32)) * gap / (gap * gap + 1.0)


def chunks_of(spg):
    cuts, at = [], 0
    while at < spg:
        size = 2 if spg - at > 3 else 1
        cuts.append((at, size))
        at += size
    return cuts


def fold(value):
    rows, cols = value.shape
    value = jnp.sum(value.reshape(rows // 8, 8, cols), axis=0)
    total = value[:, 0:128]
    for at in range(128, cols, 128):
        total = total + value[:, at:at + 128]
    return total


def coded(value, axes):
    top = jnp.maximum(jnp.max(jnp.abs(value), axis=axes, keepdims=True), 1e-30)
    code = jnp.round(value * (32767.0 / top)).astype(jnp.int32).astype(jnp.int16)
    return code, top * (1.0 / 32767.0)


def decoded(code, step):
    return code.astype(jnp.int32).astype(jnp.float32) * step


def kernel(groups, n_z, n_y, cap, rg, rs, psi, left, right, sig_o, sums_o,
           whole, lv, rv, rsend, rrecv, part, ycode, ystep, yrecv, ysrecv, zcode, zstep, zacc,
           zrecv, zsrecv, sigv,
           stat, statz, staty, statg, send_sem, recv_sem, local_sem):
    spg, rows, sec = psi.shape
    g = lax.axis_index("grp")
    o = lax.axis_index("ops")
    z, y = o // n_y, o % n_y
    count = iter(range(1 << 20))
    count_local = iter(range(1 << 20))
    sent = []

    def z_peer(d):
        return {"ops": lax.rem(z + d, n_z) * n_y + y}

    def z_from(d):
        return lax.rem(z + n_z - d, n_z)

    y_peer = {"ops": z * n_y + (n_y - 1 - y)}

    def g_peer(d):
        return {"grp": lax.rem(g + d, groups)}

    def remote(src, dst, device, arrive=None):
        i = next(count)
        copy = pltpu.make_async_remote_copy(
            src_ref=src, dst_ref=dst, send_sem=send_sem.at[i], recv_sem=recv_sem.at[i],
            device_id=device, device_id_type=MESH)
        copy.start()
        sent.append(copy)
        if arrive is None:
            return copy
        return pltpu.make_async_remote_copy(
            src_ref=src, dst_ref=arrive, send_sem=send_sem.at[i], recv_sem=recv_sem.at[i],
            device_id=device, device_id_type=MESH)

    def local(src, dst):
        copy = pltpu.make_async_copy(src, dst, local_sem.at[next(count_local)])
        copy.start()
        return copy

    def rows_of(owner):
        return pl.ds(pl.multiple_of(owner * rows, rows), rows)

    right_in = local(right.at[:, 0], rv)
    psi_in = local(psi, whole.at[:, rows_of(o)])
    left_in = local(left.at[:, 0], lv)

    barrier = pltpu.get_barrier_semaphore()
    peers = [z_peer(d) for d in range(1, n_z)] + [y_peer] + [g_peer(d) for d in range(1, groups)]
    for peer in peers:
        pl.semaphore_signal(barrier, inc=1, device_id=peer, device_id_type=MESH)
    pl.semaphore_wait(barrier, len(peers))

    from_z, from_y = {}, []
    cuts = chunks_of(spg)
    for c, (at, size) in enumerate(cuts):
        src = psi.at[pl.ds(at, size)]
        spot = whole.at[pl.ds(at, size), rows_of(o)]
        from_y.append(remote(src, spot, y_peer,
                             whole.at[pl.ds(at, size), rows_of(z * n_y + n_y - 1 - y)]))
        for d in range(1, n_z):
            from_z[c, d] = remote(src, spot, z_peer(d),
                                  whole.at[pl.ds(at, size), rows_of(z_from(d) * n_y + y)])

    right_in.wait()
    for d in range(groups):
        there = lax.rem(g + d, groups)
        found = jnp.int32(0)
        source = [jnp.int32(0)] * cap
        for j in range(spg):
            match = rg[there * spg + j] == g
            slot = rs[there * spg + j]
            for r in range(cap):
                source[r] = jnp.where(match & (found == r), slot, source[r])
            found = found + match.astype(jnp.int32)
        for r in range(cap):
            if d == 0:
                rrecv[r] = rv[source[r]]
            else:
                rsend[(d - 1) * cap + r] = rv[source[r]]
    from_g = []
    for r in range(cap):
        for d in sorted(range(1, groups), key=lambda d: abs(2 * d - groups)):
            from_g.append(remote(rsend.at[(d - 1) * cap + r], rrecv.at[d * cap + r], g_peer(d)))

    for c, (at, size) in enumerate(cuts):
        for d in range(1, n_z):
            from_z[c, d].wait_recv()
            owner = z_from(d) * n_y
            spot = whole.at[pl.ds(at, size), rows_of(owner + y)]
            from_y.append(remote(spot, spot, y_peer,
                                 whole.at[pl.ds(at, size), rows_of(owner + n_y - 1 - y)]))

    position = []
    mine = [rg[g * spg + j] for j in range(spg)]
    for j in range(spg):
        rank = jnp.int32(0)
        for i in range(j):
            rank = rank + (mine[i] == mine[j]).astype(jnp.int32)
        position.append(lax.rem(g - mine[j] + groups, groups) * cap
                        + jnp.minimum(rank, cap - 1))

    psi_in.wait()
    norm = jnp.zeros((8, 128), jnp.float32)
    for j in range(spg):
        wave = whole[j, rows_of(o), :].astype(jnp.float32)
        norm = norm + fold(wave * wave)
    stat[0, 1] = norm
    left_in.wait()
    for copy in from_g + from_y:
        copy.wait_recv()

    corr = jnp.zeros((8, 128), jnp.float32)
    across = []

    def y_out(j):
        return [remote(ystep.at[j], ysrecv.at[j], y_peer),
                remote(ycode.at[j], yrecv.at[j], y_peer)]

    for j in range(spg):
        block = whole[j]
        image = lax.dot_general(block, rrecv[position[j]], (((1,), (1,)), ((), ())),
                                preferred_element_type=jnp.float32).astype(jnp.bfloat16)
        value = jnp.dot(lv[j], image, preferred_element_type=jnp.float32)
        part[j] = value.reshape(n_z, n_y, rows, sec)
        ycode[j], ystep[j] = coded(part[j, :, n_y - 1 - y], (0, 1))
        corr = corr + fold(block.astype(jnp.float32) * value)
        if j < AHEAD:
            across.append(y_out(j))
    stat[0, 0] = corr

    def sums_out(stage):
        if stage == 0:
            return [remote(stat.at[0], statg.at[d - 1], g_peer(d)) for d in range(1, groups)]
        if stage == 1:
            return [remote(stat.at[1], statz.at[d - 1], z_peer(d)) for d in range(1, n_z)]
        return [remote(stat.at[2], staty.at[0], y_peer)]

    def sums_in(stage, copies):
        landed = (statg, statz, staty)[stage]
        for copy in copies:
            copy.wait_recv()
        total = stat[stage]
        for i in range(landed.shape[0]):
            total = total + landed[i]
        stat[stage + 1] = total

    sums = sums_out(0)
    along = []
    outs = []

    def finish(j):
        for copy in along[j]:
            copy.wait_recv()
        sigma = zacc[j, z]
        for d in range(1, n_z):
            sigma = sigma + decoded(zrecv[j, d - 1], zsrecv[j, d - 1])
        sigv[j] = sigma
        outs.append(local(sigv.at[j], sig_o.at[j]))

    done = 0
    for j in range(spg):
        for copy in across[j]:
            copy.wait_recv()
        if j in (1, 3):
            sums_in(j // 2, sums)
            sums = sums_out(j // 2 + 1)
        if j + AHEAD < spg:
            across.append(y_out(j + AHEAD))
        total = part[j, :, y] + decoded(yrecv[j], ysrecv[j])
        zacc[j] = total
        zcode[j], zstep[j] = coded(total, (1,))
        along.append([])
        for d in range(1, n_z):
            there = lax.rem(z + d, n_z)
            along[j].append(remote(zstep.at[j, there], zsrecv.at[j, d - 1], z_peer(d)))
            along[j].append(remote(zcode.at[j, there], zrecv.at[j, d - 1], z_peer(d)))
        if j > LATE:
            finish(done)
            done += 1
    sums_in(2, sums)
    outs.append(local(stat.at[3], sums_o))
    while done < spg:
        finish(done)
        done += 1
    for copy in sent:
        copy.wait_send()
    for copy in outs:
        copy.wait()


def fused_shards(psi, left_ops, right_ops, right_group, right_slot, precond_diag):
    groups = lax.axis_size("grp")
    n_y = 2
    n_z = lax.axis_size("ops") // n_y
    spg, rows, sec = psi.shape
    cap = (spg + groups - 1) // groups
    f32, bf16, i16 = jnp.float32, jnp.bfloat16, jnp.int16
    cuts = len(chunks_of(spg))
    copies = cuts * (2 * n_z - 1) + (groups - 1) * cap + 2 * spg * n_z + (n_z - 1) + 1 + (groups - 1)
    shape = jax.ShapeDtypeStruct((spg, rows, sec), f32)
    sigma, sums = pl.pallas_call(
        functools.partial(kernel, groups, n_z, n_y, cap),
        out_shape=(shape, jax.ShapeDtypeStruct((2, 8, 128), f32)),
        in_specs=[pl.BlockSpec(memory_space=pltpu.SMEM)] * 2 + [pl.BlockSpec(memory_space=pl.ANY)] * 3,
        out_specs=(pl.BlockSpec(memory_space=pl.ANY),) * 2,
        scratch_shapes=[
            pltpu.VMEM((spg, sec, sec), bf16),
            pltpu.VMEM((spg, sec, sec), bf16),
            pltpu.VMEM((spg, sec, sec), bf16),
            pltpu.VMEM(((groups - 1) * cap, sec, sec), bf16),
            pltpu.VMEM((groups * cap, sec, sec), bf16),
            pltpu.VMEM((spg, n_z, n_y, rows, sec), f32),
            pltpu.VMEM((spg, n_z, rows, sec), i16),
            pltpu.VMEM((spg, 1, 1, sec), f32),
            pltpu.VMEM((spg, n_z, rows, sec), i16),
            pltpu.VMEM((spg, 1, 1, sec), f32),
            pltpu.VMEM((spg, n_z, rows, sec), i16),
            pltpu.VMEM((spg, n_z, 1, sec), f32),
            pltpu.VMEM((spg, n_z, rows, sec), f32),
            pltpu.VMEM((spg, n_z - 1, rows, sec), i16),
            pltpu.VMEM((spg, n_z - 1, 1, sec), f32),
            pltpu.VMEM((spg, rows, sec), f32),
            pltpu.VMEM((4, 2, 8, 128), f32),
            pltpu.VMEM((n_z - 1, 2, 8, 128), f32),
            pltpu.VMEM((1, 2, 8, 128), f32),
            pltpu.VMEM((groups - 1, 2, 8, 128), f32),
            pltpu.SemaphoreType.DMA((copies,)),
            pltpu.SemaphoreType.DMA((copies,)),
            pltpu.SemaphoreType.DMA((4 + 2 * spg,)),
        ],
        compiler_params=pltpu.CompilerParams(
            collective_id=0, has_side_effects=True, vmem_limit_bytes=VMEM_BYTES),
    )(right_group.reshape(-1), right_slot, psi, left_ops, right_ops)
    return pl.pallas_call(
        correct,
        out_shape=(shape, shape),
        in_specs=[pl.BlockSpec(memory_space=pltpu.VMEM)] * 4,
        out_specs=(pl.BlockSpec(memory_space=pltpu.VMEM),) * 2,
    )(sums, sigma, psi, precond_diag)


def shards(psi, left_ops, right_ops, right_group, right_slot, precond_diag):
    spg, rows, sec = psi.shape
    groups, ops = lax.axis_size("grp"), lax.axis_size("ops")
    cap = (spg + groups - 1) // groups
    held = sec * sec * (2 * (3 * spg + (2 * groups - 1) * cap) + 4 * (3 * spg))
    fits = (rows % 16 == 0 and sec % 128 == 0 and ops % 2 == 0 and ops > 2 and groups > 1
            and spg > LATE and left_ops.shape[1] == 1 and held < 40 * 1024 * 1024)
    form = fused_shards if fits else plain_shards
    return form(psi, left_ops, right_ops, right_group, right_slot, precond_diag)


def solution(mesh):
    in_specs = (
        P("grp", "ops", None),
        P("grp", "ops", None, None),
        P("grp", "ops", None, None),
        P(),
        P(),
        P("grp", "ops", None),
    )
    out_specs = (P("grp", "ops", None), P("grp", "ops", None))
    return jax.shard_map(shards, mesh=mesh, in_specs=in_specs, out_specs=out_specs, check_vma=False)
```
